32 devices in a mesh: prompt: 1, seq: 32 (over z, y, x, core).
Axes of the slice: x: 2, y: 2, z: 4, core: 2. Of those that a mesh axis runs over, the one named last changes fastest.
Arguments:
- queries: bfloat16 [8192, 32, 128], P(('prompt', 'seq')), may hold values from -12 to 12
- key_value: bfloat16 [2, 8192, 16, 128], P(None, ('prompt', 'seq')), may hold values from -6 to 6
- damping: bfloat16 [8192], P('prompt'), may hold values from 0.0099487305 to 1
- span_start: int32 [1], P('prompt'), may hold values from 0 to 3584
- steered_heads: int32 [8], replicated, may hold values from 0 to 31, as said below
Outputs:
- attention: bfloat16 [8192, 32, 128], P(('prompt', 'seq'))
The draws below stay inside these ranges and needn't reach their ends.
Inputs may be any that keep to these rules, and one draw needn't show every extreme that they name: The emphasized tokens are span_start to span_start + 511. `steered_heads`: 8 distinct head numbers in any order; head 31 is always one of them.
All inputs are finite; a program needn't handle non-finite values.
Results may differ from the reference program's by a relative error of at most 0.0085.
Values may be sent and summed in bfloat16 or wider, within the bound.
A program may use at most 64 MiB of HBM per device.

```python
import math
import jax
import jax.numpy as jnp
from jax import lax

HEADS = 32
KV_HEADS = 16
HEAD_DIM = 128
WINDOW = 4096
SPAN = 512
STEERED = 8
TOKENS = 8192


def draw_steered_heads(key, part):
    others = jax.random.permutation(jax.random.fold_in(key, 11), HEADS - 1)[:STEERED - 1].astype(jnp.int32)
    chosen = jnp.concatenate([others, jnp.full((1,), HEADS - 1, jnp.int32)])
    order = jax.random.permutation(jax.random.fold_in(key, 23), STEERED)
    return chosen[order].astype(jnp.int32)


def shard_levels(own_key, shape, shards, least, high):
    loudness = 1.0
    for axis_at, blocks in shards:
        heights = jax.random.uniform(jax.random.fold_in(jax.random.fold_in(own_key, 6), axis_at), (blocks,), jnp.float32, least / len(shards), high / len(shards))
        loudness = loudness * jnp.repeat(jnp.exp(heights), shape[axis_at] // blocks).reshape((-1,) + (1,) * (len(shape) - 1 - axis_at))
    return loudness


def centred(rng, dims, spread, bound, split=(), held_as=jnp.bfloat16):
    factor_of = shard_levels(rng, dims, split, -0.22, 0.18) if split else 1.0
    values = jax.random.normal(rng, dims, jnp.float32) * spread * factor_of
    return jnp.minimum(jnp.maximum(values, -bound), bound).astype(held_as)


def setup_inputs(seed: int = 0, part: int = 0) -> dict:
    seeds = jax.random.split(jax.random.key(seed), 6)
    part_keys = jax.random.split(jax.random.fold_in(seeds[5], part), 6)
    queries = centred(part_keys[0], (TOKENS, HEADS, HEAD_DIM), 3.0, 12.0, ((0, 32),))
    key_value = centred(part_keys[1], (2, TOKENS, KV_HEADS, HEAD_DIM), 1.0, 6.0, ((1, 32),))
    damping = jnp.clip(jnp.exp(jax.random.uniform(part_keys[2], (TOKENS,), jnp.float32, math.log(0.0099487305), math.log(1.0))), 0.0099487305, 1.0).astype(jnp.bfloat16)
    span_start = jax.random.randint(part_keys[3], (1,), 0, max(TOKENS - WINDOW - SPAN, 0) + 1).astype(jnp.int32)
    steered_heads = draw_steered_heads(jax.random.fold_in(seeds[5], 71), part)
    return dict(queries=queries, key_value=key_value, damping=damping, span_start=span_start, steered_heads=steered_heads)


SCORE_SCALE = 144.0 ** -0.5
SOFTCAP = 50.0


def piece_terms(query_groups, key_piece, value_piece, key_bias, visible):
    raw_score = jnp.einsum("qkgd,skd->kgqs", query_groups.astype(jnp.float32), key_piece.astype(jnp.float32))
    scores = SOFTCAP * jnp.tanh(raw_score * SCORE_SCALE / SOFTCAP) + key_bias
    weight = jnp.where(visible, jnp.exp(scores), jnp.float32(0.0))
    weight_sum = jnp.sum(weight, axis=-1)
    rounded = weight.astype(jnp.bfloat16)
    weighted = jnp.einsum("kgqs,skd->kgqd", rounded.astype(jnp.float32), value_piece.astype(jnp.float32))
    return weighted, weight_sum


def reference(queries, key_value, damping, span_start, steered_heads):
    total_rows, head_count, head_width = queries.shape
    key_heads = key_value.shape[2]
    group_size = head_count // key_heads
    block_rows = min(512, total_rows)
    span_first = span_start[0].astype(jnp.int32)
    head_index = jnp.arange(head_count, dtype=jnp.int32)
    steered = jnp.any(steered_heads[:, None] == head_index[None, :], axis=0)
    steer_grid = steered.reshape(key_heads, group_size)[:, :, None, None]
    log_damping = jnp.log(damping.astype(jnp.float32))
    padded_states = jnp.pad(key_value, ((0, 0), (WINDOW, 0), (0, 0), (0, 0)))
    padded_log = jnp.pad(log_damping, (WINDOW, 0))
    span_states = lax.dynamic_slice_in_dim(key_value, span_first, SPAN, 1)
    span_index = span_first + jnp.arange(SPAN, dtype=jnp.int32)

    def one_block(block_index):
        first_row = (block_index * block_rows).astype(jnp.int32)
        query_index = first_row + jnp.arange(block_rows, dtype=jnp.int32)
        query_groups = lax.dynamic_slice_in_dim(queries, first_row, block_rows, 0).reshape(block_rows, key_heads, group_size, head_width)
        window_states = lax.dynamic_slice_in_dim(padded_states, first_row, WINDOW + block_rows, 1)
        window_log = lax.dynamic_slice_in_dim(padded_log, first_row, WINDOW + block_rows, 0)
        key_index = first_row - WINDOW + jnp.arange(WINDOW + block_rows, dtype=jnp.int32)
        emphasis = (key_index >= span_first) & (key_index < span_first + SPAN)
        distance = query_index[:, None] - key_index[None, :]
        visible = (key_index[None, :] >= 0) & (distance >= 0) & (distance < WINDOW)
        key_bias = jnp.where(steer_grid & ~emphasis[None, None, None, :], window_log[None, None, None, :], jnp.float32(0.0))
        weighted, weight_sum = piece_terms(query_groups, window_states[0], window_states[1], key_bias, visible[None, None])
        span_distance = query_index[:, None] - span_index[None, :]
        span_visible = steer_grid & (span_distance >= WINDOW)[None, None]
        more_weighted, more_sum = piece_terms(query_groups, span_states[0], span_states[1], jnp.float32(0.0), span_visible)
        result = (weighted + more_weighted) / (weight_sum + more_sum)[..., None]
        result = result.astype(jnp.bfloat16)
        return result.transpose(2, 0, 1, 3).reshape(block_rows, head_count, head_width)

    outputs = lax.map(one_block, jnp.arange(total_rows // block_rows, dtype=jnp.int32))
    return outputs.reshape(total_rows, head_count, head_width)
```

```python
import functools

import jax
import jax.numpy as jnp
from jax import lax
from jax.experimental import pallas as pl
from jax.experimental.pallas import tpu as pltpu
from jax.sharding import PartitionSpec as P

WINDOW = 4096
SPAN = 512
SCORE_SCALE = 144.0 ** (-0.5)
SOFTCAP = 50.0
LOG2E = 1.4426950408889634
BLOCK = 512


def raw_scores(q, k):
    return lax.dot_general(q, k, (((1,), (1,)), ((), ())), preferred_element_type=jnp.float32)


def weigh(raw, bias):
    capped = jnp.tanh(raw * (SCORE_SCALE / SOFTCAP)) * (SOFTCAP * LOG2E)
    return jnp.exp2(capped + bias)


def gather_values(weight, v):
    both = jnp.concatenate([v, jnp.ones_like(v)], axis=1)
    return jnp.dot(weight.astype(jnp.bfloat16), both, preferred_element_type=jnp.float32)


def attend(far_blocks, flag_ref, q_ref, k_ref, v_ref, bias_ref, sk_ref, sv_ref, out_ref, acc):
    at = pl.program_id(0)
    q = q_ref[...]
    rows = lax.broadcasted_iota(jnp.int32, (BLOCK, BLOCK), 0)
    columns = lax.broadcasted_iota(jnp.int32, (BLOCK, BLOCK), 1)
    near = columns <= rows

    def keys(block):
        return pl.ds(pl.multiple_of(block * BLOCK, BLOCK), BLOCK)

    def bias_of(block):
        return bias_ref[pl.ds(block, 1), :]

    @pl.when(at < far_blocks)
    def _():
        weight = jnp.where(near, weigh(raw_scores(q, k_ref[keys(at), :]), bias_of(at)), 0.0)
        acc[...] = gather_values(weight, v_ref[keys(at), :])

    @pl.when(at >= far_blocks)
    def _():
        far = at - far_blocks
        raw = jnp.where(
            near, raw_scores(q, k_ref[keys(at), :]), raw_scores(q, k_ref[keys(far), :])
        )
        weight = weigh(raw, jnp.where(near, bias_of(at), bias_of(far)))
        acc[...] = gather_values(
            jnp.where(near, weight, 0.0), v_ref[keys(at), :]
        ) + gather_values(jnp.where(near, 0.0, weight), v_ref[keys(far), :])

    @pl.when((at >= far_blocks) & (flag_ref[0] > 0))
    def _():
        seen = columns + flag_ref[1] + far_blocks * BLOCK <= rows + at * BLOCK
        weight = jnp.where(seen, weigh(raw_scores(q, sk_ref[...]), 0.0), 0.0)
        acc[...] += gather_values(weight, sv_ref[...])

    def whole(block):
        weight = weigh(raw_scores(q, k_ref[keys(block), :]), bias_of(block))
        return gather_values(weight, v_ref[keys(block), :])

    first = jnp.maximum(at - far_blocks + 1, 0)
    count = at - first

    @pl.loop(0, count // 2)
    def _(pair):
        acc[...] += whole(first + 2 * pair) + whole(first + 2 * pair + 1)

    @pl.when(count % 2 == 1)
    def _():
        acc[...] += whole(at - 1)

    total = acc[...]
    out_ref[...] = (total[:, :128] / total[:, 128:]).astype(out_ref.dtype)


def attention_kernel(flags, queries, keys, values, bias, span_keys, span_values):
    total_rows, width = queries.shape
    whole = lambda shape: pl.BlockSpec(
        shape, lambda i, flags: (0,) * len(shape), pipeline_mode=pl.Buffered(1)
    )
    return pl.pallas_call(
        functools.partial(attend, WINDOW // BLOCK),
        out_shape=jax.ShapeDtypeStruct((total_rows, width), jnp.bfloat16),
        grid_spec=pltpu.PrefetchScalarGridSpec(
            num_scalar_prefetch=1,
            grid=(total_rows // BLOCK,),
            in_specs=[
                pl.BlockSpec((BLOCK, width), lambda i, flags: (i, 0)),
                whole(keys.shape),
                whole(values.shape),
                whole(bias.shape),
                whole(span_keys.shape),
                whole(span_values.shape),
            ],
            out_specs=pl.BlockSpec((BLOCK, width), lambda i, flags: (i, 0)),
            scratch_shapes=[pltpu.VMEM((BLOCK, 2 * width), jnp.float32)],
        ),
        compiler_params=pltpu.CompilerParams(dimension_semantics=("arbitrary",)),
        name="attend",
    )(flags, queries, keys, values, bias, span_keys, span_values)


def per_device(queries, key_value, damping, span_start, steered_heads):
    query_rows, head_count, width = queries.shape
    key_heads = key_value.shape[2]
    total_rows = damping.shape[0]
    device = lax.axis_index("seq")
    devices = lax.axis_size("seq")
    pieces = key_value.transpose(2, 0, 1, 3).reshape(2 * key_heads, query_rows, width)
    held = lax.all_to_all(pieces, "seq", split_axis=0, concat_axis=0, tiled=True)
    held = held.reshape(total_rows, width)
    moved_queries = lax.all_to_all(
        queries.transpose(1, 0, 2), "seq", split_axis=0, concat_axis=0, tiled=True
    ).reshape(total_rows, width)
    swap = [(i, i ^ 1) for i in range(devices)]
    other = lax.ppermute(held, "seq", swap)
    odd = device % 2 == 1
    keys = jnp.where(odd, other, held)
    values = jnp.where(odd, held, other)

    span_first = span_start[0]
    steered = jnp.any(steered_heads == device)
    index = jnp.arange(total_rows, dtype=jnp.int32)
    emphasis = (index >= span_first) & (index < span_first + SPAN)
    log_damping = jnp.log(damping.astype(jnp.float32)) * LOG2E
    bias = jnp.where(steered & ~emphasis, log_damping, 0.0).reshape(-1, BLOCK)
    span_keys = lax.dynamic_slice_in_dim(keys, span_first, SPAN, 0)
    span_values = lax.dynamic_slice_in_dim(values, span_first, SPAN, 0)
    flags = jnp.stack([steered.astype(jnp.int32), span_first])
    attended = attention_kernel(
        flags, moved_queries, keys, values, bias, span_keys, span_values
    )
    back = lax.all_to_all(
        attended.reshape(devices, query_rows, width), "seq", split_axis=0, concat_axis=0, tiled=True
    )
    return back.transpose(1, 0, 2)


def solution(mesh):
    in_specs = (
        P(("prompt", "seq"), None, None),
        P(None, ("prompt", "seq"), None, None),
        P("prompt"),
        P("prompt"),
        P(),
    )
    out_specs = P(("prompt", "seq"), None, None)
    return jax.shard_map(
        per_device, mesh=mesh, in_specs=in_specs, out_specs=out_specs, check_vma=False
    )
```

```python
import functools

import jax
import jax.numpy as jnp
from jax import lax
from jax.experimental import pallas as pl
from jax.experimental.pallas import tpu as pltpu
from jax.sharding import PartitionSpec as P

WINDOW = 4096
SPAN = 512
SCORE_SCALE = 144.0 ** (-0.5)
SOFTCAP = 50.0
LOG2E = 1.4426950408889634
BLOCK = 512
PIECE = 512
PARTS = 2


def raw_scores(q, k):
    return lax.dot_general(q, k, (((1,), (1,)), ((), ())), preferred_element_type=jnp.float32)


def weigh(raw, bias):
    capped = jnp.tanh(raw * (SCORE_SCALE / SOFTCAP)) * (SOFTCAP * LOG2E)
    return jnp.exp2(capped + bias)


def gather_values(weight, v):
    both = jnp.concatenate([v, jnp.ones_like(v)], axis=1)
    return jnp.dot(weight.astype(jnp.bfloat16), both, preferred_element_type=jnp.float32)


def attend(part, sub_rows, shard_rows, flag_ref, q_ref, k_ref, v_ref, bias_ref, sk_ref, sv_ref, out_ref, acc):
    at = pl.program_id(0)
    q = q_ref[...]
    wide = bias_ref.shape[1]
    far_blocks = WINDOW // wide

    def token(shape):
        row = lax.broadcasted_iota(jnp.int32, shape, 0)
        return row // sub_rows * shard_rows + row % sub_rows + part * sub_rows

    def near_mask():
        shape = (BLOCK, wide)
        return lax.broadcasted_iota(jnp.int32, shape, 1) <= token(shape)

    def keys(block):
        return pl.ds(pl.multiple_of(block * wide, wide), wide)

    def bias_of(block):
        return bias_ref[pl.ds(block, 1), :]

    @pl.when(at < far_blocks)
    def _():
        weight = weigh(raw_scores(q, k_ref[keys(at), :]), bias_of(at))
        acc[...] = gather_values(jnp.where(near_mask(), weight, 0.0), v_ref[keys(at), :])

    @pl.when(at >= far_blocks)
    def _():
        far = at - far_blocks
        near = near_mask()
        raw = jnp.where(
            near, raw_scores(q, k_ref[keys(at), :]), raw_scores(q, k_ref[keys(far), :])
        )
        weight = weigh(raw, jnp.where(near, bias_of(at), bias_of(far)))
        acc[...] = gather_values(
            jnp.where(near, weight, 0.0), v_ref[keys(at), :]
        ) + gather_values(jnp.where(near, 0.0, weight), v_ref[keys(far), :])

    @pl.when((at >= far_blocks) & (flag_ref[0] > 0))
    def _():
        shape = (BLOCK, SPAN)
        key = lax.broadcasted_iota(jnp.int32, shape, 1) + flag_ref[1] + WINDOW
        weight = weigh(raw_scores(q, sk_ref[...]), 0.0)
        acc[...] += gather_values(
            jnp.where(key <= token(shape) + at * wide, weight, 0.0), sv_ref[...]
        )

    @pl.loop(jnp.maximum(at - far_blocks + 1, 0), at)
    def _(block):
        for piece in range(0, wide, PIECE):
            here = pl.ds(pl.multiple_of(block * wide + piece, PIECE), PIECE)
            weight = weigh(
                raw_scores(q, k_ref[here, :]), bias_ref[pl.ds(block, 1), piece : piece + PIECE]
            )
            acc[...] += gather_values(weight, v_ref[here, :])

    total = acc[...]
    out_ref[...] = (total[:, :128] / total[:, 128:]).astype(out_ref.dtype)


def attention_kernel(part, flags, queries, keys, values, bias, span_keys, span_values, shard_rows):
    part_rows, width = queries.shape
    total_rows = keys.shape[0]
    pairs = part_rows * WINDOW
    whole = lambda shape: pl.BlockSpec(
        shape, lambda i, flags: (0,) * len(shape), pipeline_mode=pl.Buffered(1)
    )
    return pl.pallas_call(
        functools.partial(attend, part, shard_rows // PARTS, shard_rows),
        out_shape=jax.ShapeDtypeStruct((part_rows, width), jnp.bfloat16),
        grid_spec=pltpu.PrefetchScalarGridSpec(
            num_scalar_prefetch=1,
            grid=(part_rows // BLOCK,),
            in_specs=[
                pl.BlockSpec((BLOCK, width), lambda i, flags: (i, 0)),
                whole(keys.shape),
                whole(values.shape),
                whole(bias.shape),
                whole(span_keys.shape),
                whole(span_values.shape),
            ],
            out_specs=pl.BlockSpec((BLOCK, width), lambda i, flags: (i, 0)),
            scratch_shapes=[pltpu.VMEM((BLOCK, 2 * width), jnp.float32)],
        ),
        compiler_params=pltpu.CompilerParams(dimension_semantics=("arbitrary",)),
        cost_estimate=pl.CostEstimate(
            flops=6 * pairs * width,
            transcendentals=2 * pairs,
            bytes_accessed=4 * (part_rows + total_rows) * width,
        ),
        name=f"attend_{part}",
    )(flags, queries, keys, values, bias, span_keys, span_values)


def per_device(queries, key_value, damping, span_start, steered_heads):
    query_rows, head_count, width = queries.shape
    key_heads = key_value.shape[2]
    total_rows = damping.shape[0]
    device = lax.axis_index("seq")
    devices = lax.axis_size("seq")
    pieces = key_value.transpose(2, 0, 1, 3).reshape(2 * key_heads, query_rows, width)
    held = lax.all_to_all(pieces, "seq", split_axis=0, concat_axis=0, tiled=True)
    held = held.reshape(total_rows, width)
    sub_rows = query_rows // PARTS
    query_pieces = [
        queries[part * sub_rows : (part + 1) * sub_rows].transpose(1, 0, 2)
        for part in range(PARTS)
    ]

    def exchange(pieces):
        return lax.all_to_all(pieces, "seq", split_axis=0, concat_axis=0, tiled=True)

    moved = [exchange(query_pieces[0])]
    swap = [(i, i ^ 1) for i in range(devices)]
    other = lax.ppermute(held, "seq", swap)
    odd = device % 2 == 1
    keys = jnp.where(odd, other, held)
    values = jnp.where(odd, held, other)

    span_first = span_start[0]
    steered = jnp.any(steered_heads == device)
    index = jnp.arange(total_rows, dtype=jnp.int32)
    emphasis = (index >= span_first) & (index < span_first + SPAN)
    log_damping = jnp.log(damping.astype(jnp.float32)) * LOG2E
    bias = jnp.where(steered & ~emphasis, log_damping, 0.0).reshape(-1, BLOCK * PARTS)
    span_keys = lax.dynamic_slice_in_dim(keys, span_first, SPAN, 0)
    span_values = lax.dynamic_slice_in_dim(values, span_first, SPAN, 0)
    flags = jnp.stack([steered.astype(jnp.int32), span_first])
    back = []
    for part in range(PARTS):
        if part + 1 < PARTS:
            later, moved[part] = lax.optimization_barrier((query_pieces[part + 1], moved[part]))
            moved.append(exchange(later))
        attended = attention_kernel(
            part,
            flags,
            moved[part].reshape(devices * sub_rows, width),
            keys,
            values,
            bias,
            span_keys,
            span_values,
            query_rows,
        )
        back.append(exchange(attended.reshape(devices, sub_rows, width)))
    return jnp.concatenate(back, axis=1).transpose(1, 0, 2)


def solution(mesh):
    in_specs = (
        P(("prompt", "seq"), None, None),
        P(None, ("prompt", "seq"), None, None),
        P("prompt"),
        P("prompt"),
        P(),
    )
    out_specs = P(("prompt", "seq"), None, None)
    return jax.shard_map(
        per_device, mesh=mesh, in_specs=in_specs, out_specs=out_specs, check_vma=False
    )
```

```python
import functools

import jax
import jax.numpy as jnp
from jax import lax
from jax.experimental import pallas as pl
from jax.experimental.pallas import tpu as pltpu
from jax.sharding import PartitionSpec as P

WINDOW = 4096
SPAN = 512
SCORE_SCALE = 144.0 ** (-0.5)
SOFTCAP = 50.0
LOG2E = 1.4426950408889634
BLOCK = 512
PIECE = 512
PARTS = 2


def raw_scores(q, k):
    return lax.dot_general(q, k, (((1,), (1,)), ((), ())), preferred_element_type=jnp.float32)


def weigh(raw, bias):
    capped = jnp.tanh(raw * (SCORE_SCALE / SOFTCAP)) * (SOFTCAP * LOG2E)
    return jnp.exp2(capped + bias)


def gather_values(weight, v):
    both = jnp.concatenate([v, jnp.ones_like(v)], axis=1)
    return jnp.dot(weight.astype(jnp.bfloat16), both, preferred_element_type=jnp.float32)


def attend(
    part, sub_rows, shard_rows, devices,
    span_ref, q_ref, k_ref, v_ref, bias_ref, sk_ref, sv_ref, out_ref,
    acc, done, send_sem, recv_sem, own_sem,
):
    me = lax.axis_index("seq")
    wide = bias_ref.shape[1]
    blocks = bias_ref.shape[0]
    far_blocks = WINDOW // wide
    shards = BLOCK // sub_rows
    barrier = pltpu.get_barrier_semaphore()

    @pl.loop(1, devices)
    def _(step):
        pl.semaphore_signal(
            barrier,
            inc=1,
            device_id={"seq": lax.rem(me + step, devices)},
            device_id_type=pl.DeviceIdType.MESH,
        )

    pl.semaphore_wait(barrier, devices - 1)

    def copy_to(target):
        return pltpu.make_async_remote_copy(
            src_ref=done.at[target],
            dst_ref=out_ref.at[me],
            send_sem=send_sem.at[target],
            recv_sem=recv_sem.at[me],
            device_id={"seq": target},
            device_id_type=pl.DeviceIdType.MESH,
        )

    def copy_own():
        return pltpu.make_async_copy(done.at[me], out_ref.at[me], own_sem)

    def token(shape):
        row = lax.broadcasted_iota(jnp.int32, shape, 0)
        return row // sub_rows * shard_rows + row % sub_rows + part * sub_rows

    def near_mask():
        shape = (BLOCK, wide)
        return lax.broadcasted_iota(jnp.int32, shape, 1) <= token(shape)

    def keys(block):
        return pl.ds(pl.multiple_of(block * wide, wide), wide)

    def bias_of(block):
        return bias_ref[pl.ds(block, 1), :]

    def block_at(step):
        return lax.rem(me // shards + step, blocks)

    def send(step):
        first = block_at(step) * shards
        for shard in range(shards):
            target = first + shard

            @pl.when(target != me)
            def _():
                copy_to(target).start()

            @pl.when(target == me)
            def _():
                copy_own().start()

    @pl.loop(0, blocks)
    def _(step):
        at = block_at(step)
        q = q_ref[pl.ds(pl.multiple_of(at * BLOCK, BLOCK), BLOCK), :]

        @pl.when(step > 0)
        def _():
            send(step - 1)

        @pl.when(at < far_blocks)
        def _():
            weight = weigh(raw_scores(q, k_ref[keys(at), :]), bias_of(at))
            acc[...] = gather_values(jnp.where(near_mask(), weight, 0.0), v_ref[keys(at), :])

        @pl.when(at >= far_blocks)
        def _():
            far = at - far_blocks
            near = near_mask()
            raw = jnp.where(
                near, raw_scores(q, k_ref[keys(at), :]), raw_scores(q, k_ref[keys(far), :])
            )
            weight = weigh(raw, jnp.where(near, bias_of(at), bias_of(far)))
            acc[...] = gather_values(
                jnp.where(near, weight, 0.0), v_ref[keys(at), :]
            ) + gather_values(jnp.where(near, 0.0, weight), v_ref[keys(far), :])
            shape = (BLOCK, SPAN)
            key = lax.broadcasted_iota(jnp.int32, shape, 1) + span_ref[...] + WINDOW
            weight = weigh(raw_scores(q, sk_ref[...]), 0.0)
            acc[...] += gather_values(
                jnp.where(key <= token(shape) + at * wide, weight, 0.0), sv_ref[...]
            )

        @pl.loop(jnp.maximum(at - far_blocks + 1, 0), at)
        def _(block):
            for piece in range(0, wide, PIECE):
                here = pl.ds(pl.multiple_of(block * wide + piece, PIECE), PIECE)
                weight = weigh(
                    raw_scores(q, k_ref[here, :]), bias_ref[pl.ds(block, 1), piece : piece + PIECE]
                )
                acc[...] += gather_values(weight, v_ref[here, :])

        total = acc[...]
        result = (total[:, :128] / total[:, 128:]).astype(done.dtype)
        done[pl.ds(at * shards, shards)] = result.reshape(shards, sub_rows, 128)

    send(blocks - 1)
    copy_own().wait()

    @pl.loop(1, devices)
    def _(step):
        other = lax.rem(me + step, devices)
        copy_to(other).wait_send()
        pltpu.make_async_remote_copy(
            src_ref=done.at[other],
            dst_ref=out_ref.at[other],
            send_sem=send_sem.at[other],
            recv_sem=recv_sem.at[other],
            device_id={"seq": other},
            device_id_type=pl.DeviceIdType.MESH,
        ).wait_recv()


def attention_kernel(part, span, queries, keys, values, bias, span_keys, span_values, devices):
    part_rows, width = queries.shape
    total_rows = keys.shape[0]
    shard_rows = total_rows // devices
    sub_rows = part_rows // devices
    pairs = part_rows * WINDOW
    return pl.pallas_call(
        functools.partial(attend, part, sub_rows, shard_rows, devices),
        out_shape=jax.ShapeDtypeStruct((devices, sub_rows, width), jnp.bfloat16),
        in_specs=[pl.BlockSpec(memory_space=pltpu.VMEM)] * 7,
        out_specs=pl.BlockSpec(memory_space=pl.ANY),
        scratch_shapes=[
            pltpu.VMEM((BLOCK, 2 * width), jnp.float32),
            pltpu.VMEM((devices, sub_rows, width), jnp.bfloat16),
            pltpu.SemaphoreType.DMA((devices,)),
            pltpu.SemaphoreType.DMA((devices,)),
            pltpu.SemaphoreType.DMA,
        ],
        compiler_params=pltpu.CompilerParams(collective_id=part, has_side_effects=True),
        cost_estimate=pl.CostEstimate(
            flops=6 * pairs * width,
            transcendentals=2 * pairs,
            bytes_accessed=4 * (part_rows + total_rows) * width,
        ),
        name=f"attend_{part}",
    )(span, queries, keys, values, bias, span_keys, span_values)


def per_device(queries, key_value, damping, span_start, steered_heads):
    query_rows, head_count, width = queries.shape
    key_heads = key_value.shape[2]
    total_rows = damping.shape[0]
    device = lax.axis_index("seq")
    devices = lax.axis_size("seq")
    pieces = key_value.transpose(2, 0, 1, 3).reshape(2 * key_heads, query_rows, width)
    held = lax.all_to_all(pieces, "seq", split_axis=0, concat_axis=0, tiled=True)
    held = held.reshape(total_rows, width)
    sub_rows = query_rows // PARTS
    query_pieces = [
        queries[part * sub_rows : (part + 1) * sub_rows].transpose(1, 0, 2)
        for part in range(PARTS)
    ]

    def exchange(pieces):
        return lax.all_to_all(pieces, "seq", split_axis=0, concat_axis=0, tiled=True)

    moved = [exchange(query_pieces[0])]
    swap = [(i, i ^ 1) for i in range(devices)]
    other = lax.ppermute(held, "seq", swap)
    odd = device % 2 == 1
    keys = jnp.where(odd, other, held)
    values = jnp.where(odd, held, other)

    span_first = span_start[0]
    steered = jnp.any(steered_heads == device)
    index = jnp.arange(total_rows, dtype=jnp.int32)
    emphasis = (index >= span_first) & (index < span_first + SPAN)
    log_damping = jnp.log(damping.astype(jnp.float32)) * LOG2E
    bias = jnp.where(steered & ~emphasis, log_damping, 0.0).reshape(-1, BLOCK * PARTS)
    span_keys = lax.dynamic_slice_in_dim(keys, span_first, SPAN, 0)
    span_values = lax.dynamic_slice_in_dim(values, span_first, SPAN, 0)
    span = jnp.where(steered, span_first, 2 * total_rows).reshape(1, 1)
    back = []
    for part in range(PARTS):
        if part + 1 < PARTS:
            later, moved[part] = lax.optimization_barrier((query_pieces[part + 1], moved[part]))
            moved.append(exchange(later))
        attended = attention_kernel(
            part,
            span,
            moved[part].reshape(devices * sub_rows, width),
            keys,
            values,
            bias,
            span_keys,
            span_values,
            devices,
        )
        back.append(attended)
    return jnp.concatenate(back, axis=1).transpose(1, 0, 2)


def solution(mesh):
    in_specs = (
        P(("prompt", "seq"), None, None),
        P(None, ("prompt", "seq"), None, None),
        P("prompt"),
        P("prompt"),
        P(),
    )
    out_specs = P(("prompt", "seq"), None, None)
    return jax.shard_map(
        per_device, mesh=mesh, in_specs=in_specs, out_specs=out_specs, check_vma=False
    )
```

```python
import functools

import jax
import jax.numpy as jnp
from jax import lax
from jax.experimental import pallas as pl
from jax.experimental.pallas import tpu as pltpu
from jax.sharding import PartitionSpec as P

WINDOW = 4096
SPAN = 512
SCORE_SCALE = 144.0 ** (-0.5)
SOFTCAP = 50.0
LOG2E = 1.4426950408889634
BLOCK = 512
PIECE = 512
PARTS = 2


def raw_scores(q, k):
    return lax.dot_general(q, k, (((1,), (1,)), ((), ())), preferred_element_type=jnp.float32)


def weigh(raw, bias):
    capped = jnp.tanh(raw * (SCORE_SCALE / SOFTCAP)) * (SOFTCAP * LOG2E)
    return jnp.exp2(capped + bias)


def gather_values(weight, v):
    both = jnp.concatenate([v, jnp.ones_like(v)], axis=1)
    return jnp.dot(weight.astype(jnp.bfloat16), both, preferred_element_type=jnp.float32)


def attend(
    part, sub_rows, shard_rows, devices,
    span_ref, q_ref, k_ref, v_ref, bias_ref, sk_ref, sv_ref, *rest,
):
    sends = part == PARTS - 1
    if sends:
        *earlier, out_ref, acc, done, send_sem, recv_sem, own_sem = rest
    else:
        done, acc = rest
    me = lax.axis_index("seq")
    wide = bias_ref.shape[1]
    blocks = bias_ref.shape[0]
    far_blocks = WINDOW // wide
    shards = BLOCK // sub_rows

    def copy_of(turn, source, target, sender):
        rows = pl.ds(turn * sub_rows, sub_rows)
        return pltpu.make_async_remote_copy(
            src_ref=source.at[target],
            dst_ref=out_ref.at[sender, rows],
            send_sem=send_sem.at[turn, target],
            recv_sem=recv_sem.at[turn, sender],
            device_id={"seq": target},
            device_id_type=pl.DeviceIdType.MESH,
        )

    def copy_own(turn, source):
        rows = pl.ds(turn * sub_rows, sub_rows)
        return pltpu.make_async_copy(source.at[me], out_ref.at[me, rows], own_sem.at[turn])

    if sends:
        barrier = pltpu.get_barrier_semaphore()

        @pl.loop(1, devices)
        def _(step):
            pl.semaphore_signal(
                barrier,
                inc=1,
                device_id={"seq": lax.rem(me + step, devices)},
                device_id_type=pl.DeviceIdType.MESH,
            )

        pl.semaphore_wait(barrier, devices - 1)
        for turn, source in enumerate(earlier):
            copy_own(turn, source).start()

            @pl.loop(1, devices)
            def _(step):
                copy_of(turn, source, lax.rem(me + step, devices), me).start()

    def token(shape):
        row = lax.broadcasted_iota(jnp.int32, shape, 0)
        return row // sub_rows * shard_rows + row % sub_rows + part * sub_rows

    def near_mask():
        shape = (BLOCK, wide)
        return lax.broadcasted_iota(jnp.int32, shape, 1) <= token(shape)

    def keys(block):
        return pl.ds(pl.multiple_of(block * wide, wide), wide)

    def bias_of(block):
        return bias_ref[pl.ds(block, 1), :]

    def block_at(step):
        return lax.rem(me // shards + step, blocks)

    def send(step):
        first = block_at(step) * shards
        for shard in range(shards):
            target = first + shard

            @pl.when(target != me)
            def _():
                copy_of(part, done, target, me).start()

            @pl.when(target == me)
            def _():
                copy_own(part, done).start()

    @pl.loop(0, blocks)
    def _(step):
        at = block_at(step)
        q = q_ref[pl.ds(pl.multiple_of(at * BLOCK, BLOCK), BLOCK), :]

        if sends:

            @pl.when(step > 0)
            def _():
                send(step - 1)

        @pl.when(at < far_blocks)
        def _():
            weight = weigh(raw_scores(q, k_ref[keys(at), :]), bias_of(at))
            acc[...] = gather_values(jnp.where(near_mask(), weight, 0.0), v_ref[keys(at), :])

        @pl.when(at >= far_blocks)
        def _():
            far = at - far_blocks
            near = near_mask()
            raw = jnp.where(
                near, raw_scores(q, k_ref[keys(at), :]), raw_scores(q, k_ref[keys(far), :])
            )
            weight = weigh(raw, jnp.where(near, bias_of(at), bias_of(far)))
            acc[...] = gather_values(
                jnp.where(near, weight, 0.0), v_ref[keys(at), :]
            ) + gather_values(jnp.where(near, 0.0, weight), v_ref[keys(far), :])
            shape = (BLOCK, SPAN)
            key = lax.broadcasted_iota(jnp.int32, shape, 1) + span_ref[...] + WINDOW
            weight = weigh(raw_scores(q, sk_ref[...]), 0.0)
            acc[...] += gather_values(
                jnp.where(key <= token(shape) + at * wide, weight, 0.0), sv_ref[...]
            )

        @pl.loop(jnp.maximum(at - far_blocks + 1, 0), at)
        def _(block):
            for piece in range(0, wide, PIECE):
                here = pl.ds(pl.multiple_of(block * wide + piece, PIECE), PIECE)
                weight = weigh(
                    raw_scores(q, k_ref[here, :]), bias_ref[pl.ds(block, 1), piece : piece + PIECE]
                )
                acc[...] += gather_values(weight, v_ref[here, :])

        total = acc[...]
        result = (total[:, :128] / total[:, 128:]).astype(done.dtype)
        done[pl.ds(at * shards, shards)] = result.reshape(shards, sub_rows, 128)

    if sends:
        send(blocks - 1)
        for turn, source in enumerate([*earlier, done]):
            copy_own(turn, source).wait()

            @pl.loop(1, devices)
            def _(step):
                other = lax.rem(me + step, devices)
                copy_of(turn, source, other, me).wait_send()
                copy_of(turn, source, other, other).wait_recv()


def attention_kernel(part, devices, earlier, span, queries, keys, values, bias, *span_states):
    part_rows, width = queries.shape
    total_rows = keys.shape[0]
    shard_rows = total_rows // devices
    sub_rows = part_rows // devices
    pairs = part_rows * WINDOW
    sends = part == PARTS - 1
    sending = [
        pltpu.VMEM((devices, sub_rows, width), jnp.bfloat16),
        pltpu.SemaphoreType.DMA((PARTS, devices)),
        pltpu.SemaphoreType.DMA((PARTS, devices)),
        pltpu.SemaphoreType.DMA((PARTS,)),
    ] if sends else []
    return pl.pallas_call(
        functools.partial(attend, part, sub_rows, shard_rows, devices),
        out_shape=jax.ShapeDtypeStruct(
            (devices, shard_rows if sends else sub_rows, width), jnp.bfloat16
        ),
        in_specs=[pl.BlockSpec(memory_space=pltpu.VMEM)] * (7 + len(earlier)),
        out_specs=pl.BlockSpec(memory_space=pl.ANY if sends else pltpu.VMEM),
        scratch_shapes=[pltpu.VMEM((BLOCK, 2 * width), jnp.float32)] + sending,
        compiler_params=pltpu.CompilerParams(
            collective_id=0 if sends else None, has_side_effects=sends
        ),
        cost_estimate=pl.CostEstimate(
            flops=6 * pairs * width,
            transcendentals=2 * pairs,
            bytes_accessed=4 * (part_rows + total_rows) * width,
        ),
        name=f"attend_{part}",
    )(span, queries, keys, values, bias, *span_states, *earlier)


def per_device(queries, key_value, damping, span_start, steered_heads):
    query_rows, head_count, width = queries.shape
    key_heads = key_value.shape[2]
    total_rows = damping.shape[0]
    device = lax.axis_index("seq")
    devices = lax.axis_size("seq")
    pieces = key_value.transpose(2, 0, 1, 3).reshape(2 * key_heads, query_rows, width)
    held = lax.all_to_all(pieces, "seq", split_axis=0, concat_axis=0, tiled=True)
    held = held.reshape(total_rows, width)
    sub_rows = query_rows // PARTS
    query_pieces = [
        queries[part * sub_rows : (part + 1) * sub_rows].transpose(1, 0, 2)
        for part in range(PARTS)
    ]

    def exchange(pieces):
        return lax.all_to_all(pieces, "seq", split_axis=0, concat_axis=0, tiled=True)

    moved = [exchange(query_pieces[0])]
    swap = [(i, i ^ 1) for i in range(devices)]
    other = lax.ppermute(held, "seq", swap)
    odd = device % 2 == 1
    keys = jnp.where(odd, other, held)
    values = jnp.where(odd, held, other)

    span_first = span_start[0]
    steered = jnp.any(steered_heads == device)
    index = jnp.arange(total_rows, dtype=jnp.int32)
    emphasis = (index >= span_first) & (index < span_first + SPAN)
    log_damping = jnp.log(damping.astype(jnp.float32)) * LOG2E
    bias = jnp.where(steered & ~emphasis, log_damping, 0.0).reshape(-1, BLOCK * PARTS)
    span_keys = lax.dynamic_slice_in_dim(keys, span_first, SPAN, 0)
    span_values = lax.dynamic_slice_in_dim(values, span_first, SPAN, 0)
    span = jnp.where(steered, span_first, 2 * total_rows).reshape(1, 1)
    earlier = []
    for part in range(PARTS):
        if part + 1 < PARTS:
            later, moved[part] = lax.optimization_barrier((query_pieces[part + 1], moved[part]))
            moved.append(exchange(later))
        attended = attention_kernel(
            part,
            devices,
            earlier,
            span,
            moved[part].reshape(devices * sub_rows, width),
            keys,
            values,
            bias,
            span_keys,
            span_values,
        )
        earlier = [*earlier, attended]
    return attended.transpose(1, 0, 2)


def solution(mesh):
    in_specs = (
        P(("prompt", "seq"), None, None),
        P(None, ("prompt", "seq"), None, None),
        P("prompt"),
        P("prompt"),
        P(),
    )
    out_specs = P(("prompt", "seq"), None, None)
    return jax.shard_map(
        per_device, mesh=mesh, in_specs=in_specs, out_specs=out_specs, check_vma=False
    )
```
